32 devices in a mesh: groups: 2 (over x), sp: 16 (over z, y, core).
Axes of the slice: x: 2, y: 2, z: 4, core: 2. Of those that a mesh axis runs over, the one named last changes fastest.
Arguments:
- fields: bfloat16 [2, 128, 64, 1440], P('groups', 'sp'), parts along dimension 0, may hold values from -6 to 6
- cotangent: bfloat16 [2, 128, 64, 1440], P('groups', None, 'sp'), parts along dimension 0, may hold values from -6 to 6
- ocean_mask: int32 [64, 1440], P('sp'), may hold values 0 or 1
- kernel: float32 [256, 7, 7], P('groups'), parts along dimension 0, may hold values from -0.875 to 0.875
- norm_gain: float32 [256], P('groups'), parts along dimension 0, may hold values from 0.25 to 1.75
- norm_shift: float32 [256], P('groups'), parts along dimension 0, may hold values from -3 to 3
- widen: bfloat16 [256, 256], P('groups'), parts along dimension 0, may hold values from -0.5 to 0.5
- hidden_offset: float32 [512], P('groups'), parts along dimension 0, may hold values from -3 to 3
- narrow: bfloat16 [256, 256], P('groups'), parts along dimension 0, may hold values from -0.375 to 0.375
- output_offset: float32 [256], P('groups'), parts along dimension 0, may hold values from -3 to 3
Outputs:
- updated: bfloat16 [2, 128, 64, 1440], P('groups', None, 'sp'), parts along dimension 0
- fields_grad: bfloat16 [2, 128, 64, 1440], P('groups', 'sp'), parts along dimension 0
- kernel_grad: float32 [256, 7, 7], P(('groups', 'sp')), parts along dimension 0
- widen_grad: float32 [256, 256], P(('groups', 'sp')), parts along dimension 0
- narrow_grad: float32 [256, 256], P(('groups', 'sp')), parts along dimension 0
- gain_grad: float32 [256], P('groups'), parts along dimension 0
- shift_grad: float32 [256], P('groups'), parts along dimension 0
- hidden_grad: float32 [512], P('groups'), parts along dimension 0
- output_grad: float32 [256], P('groups'), parts along dimension 0
The draws below stay inside these ranges and needn't reach their ends.
There are 2 independent parts, one for each index of `groups`. The reference program is written for one: setup_inputs(seed, part) draws one part's arguments, and reference() takes and returns one part's arrays. A program takes and returns all parts, laid end to end along the dimension named above; an argument that names none is the same for every part. Nothing has to cross between parts.
Inputs may be any that keep to these rules, and one draw needn't show every extreme that they name: `ocean_mask`: 1 marks an ocean cell, 0 a land cell.
All inputs are finite; a program needn't handle non-finite values. No bound on the sum of `ocean_mask` on one device may be relied on, other than what follows from the above.
Results may differ from the reference program's by a relative error of at most 0.0064.
Values may be sent and summed in bfloat16 or wider, within the bound.
A program may use at most 128 MiB of HBM per device.

```python
import math
import jax
import jax.numpy as jnp
from jax import lax

C = 128
F = 256
KS = 7
LON = 1440
SAMPLES = 1
ROWS_DEV = 4
LAT = 64


def with_ends(array, stream_key, low, high):
    index_at = [jax.random.randint(jax.random.fold_in(stream_key, axis), (), 0, length) for axis, length in enumerate(array.shape)]
    widest = array.shape.index(max(array.shape))
    beside = index_at[:widest] + [(index_at[widest] + 1) % array.shape[widest]] + index_at[widest + 1:]
    return array.at[tuple(index_at)].set(low).at[tuple(beside)].set(high)


def spiked(result, rng, source, target, blocks, factor):
    owner, partner = [(jnp.arange(result.shape[axis_at]) // (result.shape[axis_at] // blocks)).reshape([-1 if axis == axis_at else 1 for axis in range(result.ndim)]) for axis_at in (source, target)]
    chosen = jax.random.permutation(rng, blocks)[partner]
    strong = (owner == chosen) | (owner == (partner + blocks // 2) % blocks)
    return jnp.where(strong, factor * result, result)


def block_scale(rng, dims, split, least, high):
    factor_of, own = 1.0, jax.random.fold_in(rng, 6)
    for position, parts in split:
        steps = jnp.exp(jax.random.uniform(jax.random.fold_in(own, position), (parts,), jnp.float32, least / len(split), high / len(split)))
        factor_of = factor_of * jnp.repeat(steps, dims[position] // parts).reshape([-1 if axis == position else 1 for axis in range(len(dims))])
    return factor_of


def scatter_about(stream_key, dims, deviation, bound, cuts=(), kind=jnp.bfloat16):
    values = deviation * jax.random.normal(stream_key, dims, jnp.float32)
    if cuts:
        values = values * block_scale(stream_key, dims, cuts, -0.22, 0.18)
    return jnp.clip(values, -bound, bound).astype(kind)


def gaussian_with(key, extent, scale, bound, pieces, heavy, kind=jnp.bfloat16):
    values = scale * jax.random.normal(key, extent, jnp.float32)
    if pieces:
        values = values * block_scale(key, extent, pieces, -0.22, 0.18)
    return jnp.clip(spiked(values, jax.random.fold_in(key, 3), *heavy), -bound, bound).astype(kind)


def setup_inputs(seed: int = 0, part: int = 0) -> dict:
    streams_of = jax.random.split(jax.random.key(seed), 11)
    part_keys = jax.random.split(jax.random.fold_in(streams_of[10], part), 11)
    return {
        "fields": scatter_about(part_keys[0], (SAMPLES, C, LAT, LON), 1.0, 6.0, ((1, 16),)),
        "cotangent": gaussian_with(part_keys[1], (SAMPLES, C, LAT, LON), 1.0, 6.0, ((2, 16),), (2, 1, 16, 2.0)),
        "ocean_mask": with_ends((jax.random.randint(streams_of[2], (LAT, LON), 0, 4) < 3).astype(jnp.int32), jax.random.fold_in(streams_of[2], 1), 0, 1),
        "kernel": scatter_about(part_keys[3], (C, KS, KS), (KS * KS) ** -0.5, 0.875, (), jnp.float32),
        "norm_gain": jnp.clip(1.0 + 0.15 * jax.random.normal(part_keys[4], (C,), jnp.float32), 0.25, 1.75),
        "norm_shift": scatter_about(part_keys[5], (C,), 0.5, 3.0, (), jnp.float32),
        "widen": scatter_about(part_keys[6], (C, F), C ** -0.5, 0.5),
        "hidden_offset": scatter_about(part_keys[7], (F,), 0.5, 3.0, (), jnp.float32),
        "narrow": scatter_about(part_keys[8], (C, F), F ** -0.5, 0.375),
        "output_offset": scatter_about(part_keys[9], (C,), 0.5, 3.0, (), jnp.float32),
    }


EPSILON = 1e-06
PRECISE = lax.Precision.HIGHEST

def product(pattern, former, latter):
    return jnp.einsum(pattern, former.astype(jnp.float32), latter.astype(jnp.float32), precision=PRECISE)

def wrap_lon(values, rim_width):
    return jnp.concatenate([values[..., -rim_width:], values, values[..., :rim_width]], axis=-1)

def wrap_pad(values, rim_width):
    widened = wrap_lon(values, rim_width)
    return jnp.pad(widened, [(0, 0)] * (values.ndim - 2) + [(rim_width, rim_width), (0, 0)])

def apply_taps(padded, kernel_set, rows, cols):
    running = jnp.zeros(padded.shape[:2] + (rows, cols), jnp.float32)
    for row_tap in range(KS):
        for col_tap in range(KS):
            weight = kernel_set[:, row_tap, col_tap][None, :, None, None]
            running = running + weight * padded[:, :, row_tap:row_tap + rows, col_tap:col_tap + cols]
    return running

def tap_grads(padded, grads, rows, cols):
    return jnp.stack([jnp.stack([lax.optimization_barrier(jnp.sum(padded[:, :, row_tap:row_tap + rows, col_tap:col_tap + cols] * grads, axis=(0, 2, 3))) for col_tap in range(KS)], axis=-1) for row_tap in range(KS)], axis=1)

def gelu_slope(hidden):
    cdf = 0.5 * (1.0 + jax.scipy.special.erf(hidden * (1.0 / math.sqrt(2.0))))
    return cdf + hidden * jnp.exp(-0.5 * hidden * hidden) * (1.0 / math.sqrt(2.0 * math.pi))

def pointwise(conv_out, fields, cotangent, mask_rows, params):
    norm_gain, norm_shift, widen, hidden_offset, narrow, output_offset = params
    values = conv_out.astype(jnp.float32)
    centre = lax.optimization_barrier(jnp.mean(values, axis=1, keepdims=True))
    centred = values - centre
    inv_std = lax.rsqrt(lax.optimization_barrier(jnp.mean(centred * centred, axis=1, keepdims=True)) + EPSILON)
    normed = centred * inv_std
    scaled = (normed * norm_gain[None, :, None, None] + norm_shift[None, :, None, None]).astype(jnp.bfloat16)
    hidden = product('schw,cf->sfhw', scaled, widen) + hidden_offset[None, :, None, None]
    active = jax.nn.gelu(hidden, approximate=False).astype(jnp.bfloat16)
    branch = product('sfhw,cf->schw', active, narrow) + output_offset[None, :, None, None]
    ocean_rows = mask_rows.astype(jnp.float32)[None, None]
    updated = (fields.astype(jnp.float32) + ocean_rows * branch).astype(jnp.bfloat16)
    upstream = (cotangent.astype(jnp.float32) * ocean_rows).astype(jnp.bfloat16)
    output_part = lax.optimization_barrier(jnp.sum(upstream.astype(jnp.float32), axis=(0, 2, 3)))
    narrow_part = product('schw,sfhw->cf', upstream, active)
    active_back = product('schw,cf->sfhw', upstream, narrow)
    hidden_back = (active_back * gelu_slope(hidden)).astype(jnp.bfloat16)
    hidden_part = lax.optimization_barrier(jnp.sum(hidden_back.astype(jnp.float32), axis=(0, 2, 3)))
    widen_part = product('schw,sfhw->cf', scaled, hidden_back)
    scaled_back = product('sfhw,cf->schw', hidden_back, widen)
    gain_part = lax.optimization_barrier(jnp.sum(scaled_back * normed, axis=(0, 2, 3)))
    shift_part = lax.optimization_barrier(jnp.sum(scaled_back, axis=(0, 2, 3)))
    normed_back = scaled_back * norm_gain[None, :, None, None]
    conv_back = inv_std * (normed_back - lax.optimization_barrier(jnp.mean(normed_back, axis=1, keepdims=True)) - normed * lax.optimization_barrier(jnp.mean(normed_back * normed, axis=1, keepdims=True)))
    return (updated, conv_back.astype(jnp.bfloat16), (widen_part, narrow_part, gain_part, shift_part, hidden_part, output_part))

def reference(fields, cotangent, ocean_mask, kernel, norm_gain, norm_shift, widen, hidden_offset, narrow, output_offset):
    params = (norm_gain, norm_shift, widen, hidden_offset, narrow, output_offset)
    rim_width = KS // 2
    grad_scale = 1.0 / math.sqrt(SAMPLES * LAT * LON)
    by_channel = jnp.moveaxis(fields, 1, 0)

    def forward_conv(inputs):
        channel_plane, kernel_one = inputs
        padded = wrap_pad(channel_plane[:, None].astype(jnp.float32), rim_width)
        return apply_taps(padded, kernel_one[None], LAT, LON)[:, 0].astype(jnp.bfloat16)
    conv_out = jnp.moveaxis(lax.map(forward_conv, (by_channel, kernel)), 0, 1)
    blocks = LAT // ROWS_DEV

    def one_block(totals, block_index):
        first_row = (block_index * ROWS_DEV).astype(jnp.int32)

        def take_rows(source):
            return lax.dynamic_slice_in_dim(source, first_row, ROWS_DEV, 2)
        mask_rows = lax.dynamic_slice_in_dim(ocean_mask, first_row, ROWS_DEV, 0)
        updated, conv_back, partials = pointwise(take_rows(conv_out), take_rows(fields), take_rows(cotangent), mask_rows, params)
        return (tuple((running + extra for running, extra in zip(totals, partials))), (updated, conv_back))
    starts = (jnp.zeros((C, F), jnp.float32), jnp.zeros((C, F), jnp.float32), jnp.zeros((C,), jnp.float32), jnp.zeros((C,), jnp.float32), jnp.zeros((F,), jnp.float32), jnp.zeros((C,), jnp.float32))
    totals, (updated_blocks, back_blocks) = lax.scan(one_block, starts, jnp.arange(blocks, dtype=jnp.int32))
    updated = jnp.moveaxis(updated_blocks, 0, 2).reshape(SAMPLES, C, LAT, LON)
    conv_back = jnp.moveaxis(back_blocks, 0, 2).reshape(SAMPLES, C, LAT, LON)

    def backward_conv(inputs):
        channel_plane, grad_plane, upstream_plane, kernel_one = inputs
        padded = wrap_pad(channel_plane[:, None].astype(jnp.float32), rim_width)
        grad_values = grad_plane[:, None].astype(jnp.float32)
        kernel_part = tap_grads(padded, grad_values, LAT, LON)[0]
        spread = apply_taps(wrap_pad(grad_values, rim_width), kernel_one[None, ::-1, ::-1], LAT, LON)[:, 0]
        return (kernel_part, (upstream_plane.astype(jnp.float32) + spread).astype(jnp.bfloat16))
    kernel_sum, grad_planes = lax.map(backward_conv, (by_channel, jnp.moveaxis(conv_back, 1, 0), jnp.moveaxis(cotangent, 1, 0), kernel))
    fields_grad = jnp.moveaxis(grad_planes, 0, 1)
    widen_sum, narrow_sum, gain_sum, shift_sum, hidden_sum, output_sum = totals
    return (updated, fields_grad, kernel_sum * grad_scale, widen_sum * grad_scale, narrow_sum * grad_scale, gain_sum * grad_scale, shift_sum * grad_scale, hidden_sum * grad_scale, output_sum * grad_scale)
```

```python
import functools
import math

import jax
import jax.numpy as jnp
import numpy as np
from jax import lax
from jax.experimental import pallas as pl
from jax.experimental.pallas import tpu as pltpu
from jax.sharding import PartitionSpec as P

KS = 7
RIM = KS // 2
EPSILON = 1e-06
GROUP = 16
NT = (((1,), (1,)), ((), ()))


def dot(former, latter):
    return jnp.dot(former, latter, preferred_element_type=jnp.float32)


def dot_nt(former, latter):
    return lax.dot_general(former, latter, NT, preferred_element_type=jnp.float32)


def band_matrix(kernel, rows):
    channels = kernel.shape[0]
    taps = jnp.swapaxes(kernel, 1, 2)
    shifted = jnp.stack([jnp.pad(taps, ((0, 0), (0, 0), (h, rows - 1 - h))) for h in range(rows)])
    span = KS * (rows + KS - 1)
    shifted = shifted.reshape(rows, channels, span).astype(jnp.bfloat16)
    spread = jnp.asarray(np.repeat(np.eye(span, dtype=np.float32), GROUP, axis=1), jnp.bfloat16)
    wide = jnp.einsum("hck,kn->hcn", shifted, spread, preferred_element_type=jnp.float32)
    same = (jnp.arange(channels)[:, None] % GROUP) == (jnp.arange(span * GROUP)[None, :] % GROUP)
    return jnp.where(same[None], wide, 0.0).astype(jnp.bfloat16)


def shifts(values, scratch):
    rows, group, lon = values.shape
    flat = values.reshape(rows * group, lon)
    wrapped = jnp.concatenate([flat[:, -RIM:], flat, flat[:, :RIM]], axis=1)
    for tap in range(KS):
        scratch[tap * rows * group : (tap + 1) * rows * group, :] = wrapped[:, tap : tap + lon]


def conv_kernel(above, own, below, band, out, scratch):
    rows, group, lon = own.shape
    shifts(jnp.concatenate([above[...], own[...], below[...]], axis=0), scratch)
    result = dot(band[...].reshape(rows * group, -1), scratch[...])
    out[...] = result.astype(out.dtype).reshape(rows, group, lon)


def back_kernel(x_above, x_own, x_below, g_above, g_own, g_below, cotangent, band, out, parts, scratch):
    rows, group, lon = x_own.shape
    grads = g_own[...].reshape(rows * group, lon)
    shifts(jnp.concatenate([x_above[...], x_own[...], x_below[...]], axis=0), scratch)
    pairs = dot_nt(grads, scratch[...])
    row = lax.broadcasted_iota(jnp.int32, pairs.shape, 0) % group
    col = lax.broadcasted_iota(jnp.int32, pairs.shape, 1) % group
    kept = jnp.where(row == col, pairs, 0.0)
    parts[...] = jnp.sum(kept.reshape(rows, group, -1), axis=1)[None]
    shifts(jnp.concatenate([g_above[...], g_own[...], g_below[...]], axis=0), scratch)
    spread = dot(band[...].reshape(rows * group, -1), scratch[...])
    total = cotangent[...].reshape(rows * group, lon).astype(jnp.float32) + spread
    out[...] = total.astype(out.dtype).reshape(rows, group, lon)


def pointwise_kernel(
    conv, fields, cotangent, mask, gain, shift, widen, widen_t, hidden_off, narrow, narrow_t, out_off,
    updated, conv_back, widen_part, narrow_part, gain_part, shift_part, hidden_part, out_part,
):
    lon = conv.shape[-1]

    @pl.when(pl.program_id(0) == 0)
    def _():
        for part in (widen_part, narrow_part, gain_part, shift_part, hidden_part, out_part):
            part[...] = jnp.zeros_like(part)

    f32, bf16 = jnp.float32, jnp.bfloat16
    step = 256
    for first in range(0, lon, step):
        cols = slice(first, min(first + step, lon))
        values = conv[0, :, cols].astype(f32)
        centre = jnp.mean(values, axis=0, keepdims=True)
        centred = values - centre
        inv_std = lax.rsqrt(jnp.mean(centred * centred, axis=0, keepdims=True) + EPSILON)
        normed = centred * inv_std
        scaled = (normed * gain[...] + shift[...]).astype(bf16)
        hidden = dot(widen_t[...], scaled) + hidden_off[...]
        cdf = 0.5 * (1.0 + lax.erf(hidden * (1.0 / math.sqrt(2.0))))
        active = (hidden * cdf).astype(bf16)
        slope = cdf + hidden * jnp.exp(-0.5 * hidden * hidden) * (1.0 / math.sqrt(2.0 * math.pi))
        ocean = mask[0, :, cols].astype(f32)
        branch = dot(narrow[...], active) + out_off[...]
        updated[0, :, cols] = (fields[0, :, cols].astype(f32) + ocean * branch).astype(bf16)
        upstream_wide = cotangent[0, :, cols].astype(f32) * ocean
        upstream = upstream_wide.astype(bf16)
        out_part[...] += jnp.sum(upstream_wide, axis=1, keepdims=True)
        narrow_part[...] += dot_nt(upstream, active)
        hidden_wide = dot(narrow_t[...], upstream) * slope
        hidden_back = hidden_wide.astype(bf16)
        hidden_part[...] += jnp.sum(hidden_wide, axis=1, keepdims=True)
        widen_part[...] += dot_nt(scaled, hidden_back)
        scaled_back = dot(widen[...], hidden_back)
        gain_part[...] += jnp.sum(scaled_back * normed, axis=1, keepdims=True)
        shift_part[...] += jnp.sum(scaled_back, axis=1, keepdims=True)
        normed_back = scaled_back * gain[...]
        conv_back[0, :, cols] = (
            inv_std
            * (
                normed_back
                - jnp.mean(normed_back, axis=0, keepdims=True)
                - normed * jnp.mean(normed_back * normed, axis=0, keepdims=True)
            )
        ).astype(bf16)


def halos(values, devices):
    above = lax.ppermute(values[-RIM:], "sp", [(d, d + 1) for d in range(devices - 1)])
    below = lax.ppermute(values[:RIM], "sp", [(d + 1, d) for d in range(devices - 1)])
    return above, below


def local(
    fields, cotangent, ocean_mask, kernel, norm_gain, norm_shift, widen, hidden_offset, narrow, output_offset
):
    devices = lax.axis_size("sp")
    samples, channels, rows, lon = cotangent.shape
    wide = widen.shape[1]
    f32, bf16 = jnp.float32, jnp.bfloat16
    grad_scale = 1.0 / math.sqrt(samples * rows * devices * lon)
    groups = channels // GROUP
    span = KS * (rows + KS - 1) * GROUP
    params = pltpu.CompilerParams(vmem_limit_bytes=48 * 1024 * 1024)

    band = band_matrix(kernel, rows)
    band_back = band_matrix(kernel[:, ::-1, ::-1], rows)
    cot_rows = jnp.swapaxes(cotangent[0], 0, 1)

    own = lax.all_to_all(fields, "sp", split_axis=2, concat_axis=1, tiled=True)
    own = jnp.swapaxes(own[0], 0, 1)
    above, below = halos(own, devices)

    def rows_spec(count):
        return pl.BlockSpec((count, GROUP, lon), lambda g: (0, g, 0))

    band_spec = pl.BlockSpec((rows, GROUP, span), lambda g: (0, g, 0))
    conv_out = pl.pallas_call(
        conv_kernel,
        name="depthwise",
        grid=(groups,),
        in_specs=[rows_spec(RIM), rows_spec(rows), rows_spec(RIM), band_spec],
        out_specs=rows_spec(rows),
        out_shape=jax.ShapeDtypeStruct((rows, channels, lon), bf16),
        scratch_shapes=[pltpu.VMEM((span, lon), bf16)],
        compiler_params=params,
    )(above, own, below, band)

    def row_spec(count):
        return pl.BlockSpec((1, count, lon), lambda h: (h, 0, 0))

    def whole(*shape):
        return pl.BlockSpec(shape, lambda h: (0,) * len(shape))

    column = lambda vector: vector[:, None]
    updated, conv_back, widen_part, narrow_part, gain_part, shift_part, hidden_part, out_part = pl.pallas_call(
        pointwise_kernel,
        name="pointwise",
        grid=(rows,),
        in_specs=[
            row_spec(channels), row_spec(channels), row_spec(channels), row_spec(1),
            whole(channels, 1), whole(channels, 1), whole(channels, wide), whole(wide, channels),
            whole(wide, 1), whole(channels, wide), whole(wide, channels), whole(channels, 1),
        ],
        out_specs=[
            row_spec(channels), row_spec(channels), whole(channels, wide), whole(channels, wide),
            whole(channels, 1), whole(channels, 1), whole(wide, 1), whole(channels, 1),
        ],
        out_shape=[
            jax.ShapeDtypeStruct((rows, channels, lon), bf16),
            jax.ShapeDtypeStruct((rows, channels, lon), bf16),
            jax.ShapeDtypeStruct((channels, wide), f32),
            jax.ShapeDtypeStruct((channels, wide), f32),
            jax.ShapeDtypeStruct((channels, 1), f32),
            jax.ShapeDtypeStruct((channels, 1), f32),
            jax.ShapeDtypeStruct((wide, 1), f32),
            jax.ShapeDtypeStruct((channels, 1), f32),
        ],
        compiler_params=params,
    )(
        conv_out, own, cot_rows, ocean_mask[:, None, :], column(norm_gain), column(norm_shift),
        widen, widen.T, column(hidden_offset), narrow, narrow.T, column(output_offset),
    )

    g_above, g_below = halos(conv_back, devices)
    grad_rows, pairs = pl.pallas_call(
        back_kernel,
        name="depthwise_back",
        grid=(groups,),
        in_specs=[
            rows_spec(RIM), rows_spec(rows), rows_spec(RIM),
            rows_spec(RIM), rows_spec(rows), rows_spec(RIM),
            rows_spec(rows), band_spec,
        ],
        out_specs=[rows_spec(rows), pl.BlockSpec((1, rows, span), lambda g: (g, 0, 0))],
        out_shape=[
            jax.ShapeDtypeStruct((rows, channels, lon), bf16),
            jax.ShapeDtypeStruct((groups, rows, span), f32),
        ],
        scratch_shapes=[pltpu.VMEM((span, lon), bf16)],
        compiler_params=params,
    )(above, own, below, g_above, conv_back, g_below, cot_rows, band_back)

    fields_grad = lax.all_to_all(
        jnp.swapaxes(grad_rows, 0, 1)[None], "sp", split_axis=1, concat_axis=2, tiled=True
    )

    pairs = pairs.reshape(groups, rows, KS, rows + KS - 1, GROUP)
    taps = sum(pairs[:, h, :, h : h + KS, :] for h in range(rows))
    kernel_part = jnp.transpose(taps, (0, 3, 2, 1)).reshape(channels, KS * KS)
    tail = -(2 * wide + KS * KS) % 128
    joined = jnp.concatenate(
        [widen_part, narrow_part, kernel_part, jnp.zeros((channels, tail), f32)], axis=1
    )
    summed = lax.psum_scatter(joined, "sp", scatter_dimension=0, tiled=True) * grad_scale
    small = jnp.concatenate([gain_part[:, 0], shift_part[:, 0], hidden_part[:, 0], out_part[:, 0]])
    small = jnp.sum(lax.all_gather(small, "sp"), axis=0) * grad_scale
    edges = np.cumsum([channels, channels, wide])
    gain_sum, shift_sum, hidden_sum, output_sum = jnp.split(small, edges)
    return (
        jnp.swapaxes(updated, 0, 1)[None],
        fields_grad,
        summed[:, 2 * wide : 2 * wide + KS * KS].reshape(-1, KS, KS),
        summed[:, :wide],
        summed[:, wide : 2 * wide],
        gain_sum,
        shift_sum,
        hidden_sum,
        output_sum,
    )


def solution(mesh):
    return jax.shard_map(
        local,
        mesh=mesh,
        in_specs=(
            P("groups", "sp", None, None),
            P("groups", None, "sp", None),
            P("sp", None),
            P("groups", None, None),
            P("groups"),
            P("groups"),
            P("groups", None),
            P("groups"),
            P("groups", None),
            P("groups"),
        ),
        out_specs=(
            P("groups", None, "sp", None),
            P("groups", "sp", None, None),
            P(("groups", "sp"), None, None),
            P(("groups", "sp"), None),
            P(("groups", "sp"), None),
            P("groups"),
            P("groups"),
            P("groups"),
            P("groups"),
        ),
        check_vma=False,
    )
```

```python
import functools
import math

import jax
import jax.numpy as jnp
import numpy as np
from jax import lax
from jax.experimental import pallas as pl
from jax.experimental.pallas import tpu as pltpu
from jax.sharding import PartitionSpec as P

KS = 7
RIM = KS // 2
EPSILON = 1e-06
GROUP = 16
NT = (((1,), (1,)), ((), ()))


def dot(former, latter):
    return jnp.dot(former, latter, preferred_element_type=jnp.float32)


def dot_nt(former, latter):
    return lax.dot_general(former, latter, NT, preferred_element_type=jnp.float32)


def band_matrix(kernel, rows):
    channels = kernel.shape[0]
    taps = jnp.swapaxes(kernel, 1, 2)
    shifted = jnp.stack([jnp.pad(taps, ((0, 0), (0, 0), (h, rows - 1 - h))) for h in range(rows)])
    span = KS * (rows + KS - 1)
    shifted = shifted.reshape(rows, channels, span).astype(jnp.bfloat16)
    spread = jnp.asarray(np.repeat(np.eye(span, dtype=np.float32), GROUP, axis=1), jnp.bfloat16)
    wide = jnp.einsum("hck,kn->hcn", shifted, spread, preferred_element_type=jnp.float32)
    same = (jnp.arange(channels)[:, None] % GROUP) == (jnp.arange(span * GROUP)[None, :] % GROUP)
    return jnp.where(same[None], wide, 0.0).astype(jnp.bfloat16)


def shifts(values, scratch):
    rows, group, lon = values.shape
    flat = values.reshape(rows * group, lon)
    wrapped = jnp.concatenate([flat[:, -RIM:], flat, flat[:, :RIM]], axis=1)
    for tap in range(KS):
        scratch[tap * rows * group : (tap + 1) * rows * group, :] = wrapped[:, tap : tap + lon]


def conv_kernel(above, own, below, band, out, scratch):
    rows, group, lon = own.shape
    shifts(jnp.concatenate([above[...], own[...], below[...]], axis=0), scratch)
    result = dot(band[...].reshape(rows * group, -1), scratch[...])
    out[...] = result.astype(out.dtype).reshape(rows, group, lon)


def tap_kernel(above, own, below, grads, parts, scratch):
    rows, group, lon = own.shape
    shifts(jnp.concatenate([above[...], own[...], below[...]], axis=0), scratch)
    pairs = dot_nt(grads[...].reshape(rows * group, lon), scratch[...])
    row = lax.broadcasted_iota(jnp.int32, pairs.shape, 0) % group
    col = lax.broadcasted_iota(jnp.int32, pairs.shape, 1) % group
    kept = jnp.where(row == col, pairs, 0.0)
    parts[...] = jnp.sum(kept.reshape(rows, group, -1), axis=1)[None]


def back_kernel(above, own, below, cotangent, band, out, scratch):
    rows, group, lon = own.shape
    shifts(jnp.concatenate([above[...], own[...], below[...]], axis=0), scratch)
    spread = dot(band[...].reshape(rows * group, -1), scratch[...])
    total = cotangent[...].reshape(rows * group, lon).astype(jnp.float32) + spread
    out[...] = total.astype(out.dtype).reshape(rows, group, lon)


def pointwise_kernel(
    conv, fields, cotangent, mask, gain, shift, widen, widen_t, hidden_off, narrow, narrow_t, out_off,
    updated, conv_back, widen_part, narrow_part, gain_part, shift_part, hidden_part, out_part,
):
    lon = conv.shape[-1]

    @pl.when(pl.program_id(0) == 0)
    def _():
        for part in (widen_part, narrow_part, gain_part, shift_part, hidden_part, out_part):
            part[...] = jnp.zeros_like(part)

    f32, bf16 = jnp.float32, jnp.bfloat16
    step = 256
    for first in range(0, lon, step):
        cols = slice(first, min(first + step, lon))
        values = conv[0, :, cols].astype(f32)
        centre = jnp.mean(values, axis=0, keepdims=True)
        centred = values - centre
        inv_std = lax.rsqrt(jnp.mean(centred * centred, axis=0, keepdims=True) + EPSILON)
        normed = centred * inv_std
        scaled = (normed * gain[...] + shift[...]).astype(bf16)
        hidden = dot(widen_t[...], scaled) + hidden_off[...]
        cdf = 0.5 * (1.0 + lax.erf(hidden * (1.0 / math.sqrt(2.0))))
        active = (hidden * cdf).astype(bf16)
        slope = cdf + hidden * jnp.exp(-0.5 * hidden * hidden) * (1.0 / math.sqrt(2.0 * math.pi))
        ocean = mask[0, :, cols].astype(f32)
        branch = dot(narrow[...], active) + out_off[...]
        updated[0, :, cols] = (fields[0, :, cols].astype(f32) + ocean * branch).astype(bf16)
        upstream_wide = cotangent[0, :, cols].astype(f32) * ocean
        upstream = upstream_wide.astype(bf16)
        out_part[...] += jnp.sum(upstream_wide, axis=1, keepdims=True)
        narrow_part[...] += dot_nt(upstream, active)
        hidden_wide = dot(narrow_t[...], upstream) * slope
        hidden_back = hidden_wide.astype(bf16)
        hidden_part[...] += jnp.sum(hidden_wide, axis=1, keepdims=True)
        widen_part[...] += dot_nt(scaled, hidden_back)
        scaled_back = dot(widen[...], hidden_back)
        gain_part[...] += jnp.sum(scaled_back * normed, axis=1, keepdims=True)
        shift_part[...] += jnp.sum(scaled_back, axis=1, keepdims=True)
        normed_back = scaled_back * gain[...]
        conv_back[0, :, cols] = (
            inv_std
            * (
                normed_back
                - jnp.mean(normed_back, axis=0, keepdims=True)
                - normed * jnp.mean(normed_back * normed, axis=0, keepdims=True)
            )
        ).astype(bf16)


def halos(values, devices):
    above = lax.ppermute(values[-RIM:], "sp", [(d, d + 1) for d in range(devices - 1)])
    below = lax.ppermute(values[:RIM], "sp", [(d + 1, d) for d in range(devices - 1)])
    return above, below


def local(
    fields, cotangent, ocean_mask, kernel, norm_gain, norm_shift, widen, hidden_offset, narrow, output_offset
):
    devices = lax.axis_size("sp")
    samples, channels, rows, lon = cotangent.shape
    wide = widen.shape[1]
    f32, bf16 = jnp.float32, jnp.bfloat16
    grad_scale = 1.0 / math.sqrt(samples * rows * devices * lon)
    groups = channels // GROUP
    span = KS * (rows + KS - 1) * GROUP
    cost = pl.CostEstimate(
        flops=2 * rows * GROUP * span * lon * groups, bytes_accessed=4 * rows * channels * lon * 3, transcendentals=0
    )
    params = pltpu.CompilerParams(vmem_limit_bytes=48 * 1024 * 1024)

    band = band_matrix(kernel, rows)
    band_back = band_matrix(kernel[:, ::-1, ::-1], rows)
    cot_rows = jnp.swapaxes(cotangent[0], 0, 1)

    own = lax.all_to_all(fields, "sp", split_axis=2, concat_axis=1, tiled=True)
    own = jnp.swapaxes(own[0], 0, 1)
    above, below = halos(own, devices)

    def rows_spec(count):
        return pl.BlockSpec((count, GROUP, lon), lambda g: (0, g, 0))

    band_spec = pl.BlockSpec((rows, GROUP, span), lambda g: (0, g, 0))
    conv_out = pl.pallas_call(
        conv_kernel,
        name="depthwise",
        grid=(groups,),
        in_specs=[rows_spec(RIM), rows_spec(rows), rows_spec(RIM), band_spec],
        out_specs=rows_spec(rows),
        out_shape=jax.ShapeDtypeStruct((rows, channels, lon), bf16),
        scratch_shapes=[pltpu.VMEM((span, lon), bf16)],
        compiler_params=params,
    )(above, own, below, band)

    def row_spec(count):
        return pl.BlockSpec((1, count, lon), lambda h: (h, 0, 0))

    def whole(*shape):
        return pl.BlockSpec(shape, lambda h: (0,) * len(shape))

    column = lambda vector: vector[:, None]
    updated, conv_back, widen_part, narrow_part, gain_part, shift_part, hidden_part, out_part = pl.pallas_call(
        pointwise_kernel,
        name="pointwise",
        grid=(rows,),
        in_specs=[
            row_spec(channels), row_spec(channels), row_spec(channels), row_spec(1),
            whole(channels, 1), whole(channels, 1), whole(channels, wide), whole(wide, channels),
            whole(wide, 1), whole(channels, wide), whole(wide, channels), whole(channels, 1),
        ],
        out_specs=[
            row_spec(channels), row_spec(channels), whole(channels, wide), whole(channels, wide),
            whole(channels, 1), whole(channels, 1), whole(wide, 1), whole(channels, 1),
        ],
        out_shape=[
            jax.ShapeDtypeStruct((rows, channels, lon), bf16),
            jax.ShapeDtypeStruct((rows, channels, lon), bf16),
            jax.ShapeDtypeStruct((channels, wide), f32),
            jax.ShapeDtypeStruct((channels, wide), f32),
            jax.ShapeDtypeStruct((channels, 1), f32),
            jax.ShapeDtypeStruct((channels, 1), f32),
            jax.ShapeDtypeStruct((wide, 1), f32),
            jax.ShapeDtypeStruct((channels, 1), f32),
        ],
        compiler_params=params,
    )(
        conv_out, own, cot_rows, ocean_mask[:, None, :], column(norm_gain), column(norm_shift),
        widen, widen.T, column(hidden_offset), narrow, narrow.T, column(output_offset),
    )

    g_above, g_below = halos(conv_back, devices)
    pairs = pl.pallas_call(
        tap_kernel,
        name="tap_grads",
        grid=(groups,),
        in_specs=[rows_spec(RIM), rows_spec(rows), rows_spec(RIM), rows_spec(rows)],
        out_specs=pl.BlockSpec((1, rows, span), lambda g: (g, 0, 0)),
        out_shape=jax.ShapeDtypeStruct((groups, rows, span), f32),
        scratch_shapes=[pltpu.VMEM((span, lon), bf16)],
        compiler_params=params,
        cost_estimate=cost,
    )(above, own, below, conv_back)

    pairs = pairs.reshape(groups, rows, KS, rows + KS - 1, GROUP)
    taps = sum(pairs[:, h, :, h : h + KS, :] for h in range(rows))
    kernel_part = jnp.transpose(taps, (0, 3, 2, 1)).reshape(channels, KS * KS)
    small = jnp.concatenate([gain_part[:, 0], shift_part[:, 0], hidden_part[:, 0], out_part[:, 0]])
    pieces = [
        part.reshape(devices, -1)
        for part in (widen_part, narrow_part, jnp.pad(kernel_part, ((0, 0), (0, 128 - KS * KS))))
    ]
    pieces.append(jnp.broadcast_to(small[None], (devices, small.shape[0])))
    joined = jnp.concatenate([piece.reshape(devices, -1, 128) for piece in pieces], axis=1)
    joined = lax.all_to_all(joined, "sp", split_axis=0, concat_axis=0, tiled=True)
    summed = jnp.sum(joined, axis=0) * grad_scale

    grad_rows = pl.pallas_call(
        back_kernel,
        name="depthwise_back",
        grid=(groups,),
        in_specs=[rows_spec(RIM), rows_spec(rows), rows_spec(RIM), rows_spec(rows), band_spec],
        out_specs=rows_spec(rows),
        out_shape=jax.ShapeDtypeStruct((rows, channels, lon), bf16),
        scratch_shapes=[pltpu.VMEM((span, lon), bf16)],
        compiler_params=params,
        cost_estimate=cost,
    )(g_above, conv_back, g_below, cot_rows, band_back)

    fields_grad = lax.all_to_all(
        jnp.swapaxes(grad_rows, 0, 1)[None], "sp", split_axis=1, concat_axis=2, tiled=True
    )

    own_channels = channels // devices
    edges = np.cumsum([own_channels * wide // 128, own_channels * wide // 128, own_channels])
    widen_sum, narrow_sum, kernel_sum, small_sum = jnp.split(summed, edges)
    small_sum = small_sum.reshape(-1)
    gain_sum, shift_sum, hidden_sum, output_sum = jnp.split(small_sum, np.cumsum([channels, channels, wide]))
    return (
        jnp.swapaxes(updated, 0, 1)[None],
        fields_grad,
        kernel_sum[:, : KS * KS].reshape(-1, KS, KS),
        widen_sum.reshape(-1, wide),
        narrow_sum.reshape(-1, wide),
        gain_sum,
        shift_sum,
        hidden_sum,
        output_sum,
    )


def solution(mesh):
    return jax.shard_map(
        local,
        mesh=mesh,
        in_specs=(
            P("groups", "sp", None, None),
            P("groups", None, "sp", None),
            P("sp", None),
            P("groups", None, None),
            P("groups"),
            P("groups"),
            P("groups", None),
            P("groups"),
            P("groups", None),
            P("groups"),
        ),
        out_specs=(
            P("groups", None, "sp", None),
            P("groups", "sp", None, None),
            P(("groups", "sp"), None, None),
            P(("groups", "sp"), None),
            P(("groups", "sp"), None),
            P("groups"),
            P("groups"),
            P("groups"),
            P("groups"),
        ),
        check_vma=False,
    )
```

```python
import functools
import math

import jax
import jax.numpy as jnp
import numpy as np
from jax import lax
from jax.experimental import pallas as pl
from jax.experimental.layout import Layout, with_layout_constraint
from jax.experimental.pallas import tpu as pltpu
from jax.sharding import PartitionSpec as P

KS = 7
RIM = KS // 2
EPSILON = 1e-06
GROUP = 16
NT = (((1,), (1,)), ((), ()))


def dot(former, latter):
    return jnp.dot(former, latter, preferred_element_type=jnp.float32)


def dot_nt(former, latter):
    return lax.dot_general(former, latter, NT, preferred_element_type=jnp.float32)


def band_matrix(kernel, rows):
    channels = kernel.shape[0]
    taps = jnp.swapaxes(kernel, 1, 2)
    shifted = jnp.stack([jnp.pad(taps, ((0, 0), (0, 0), (h, rows - 1 - h))) for h in range(rows)])
    span = KS * (rows + KS - 1)
    shifted = shifted.reshape(rows, channels, span).astype(jnp.bfloat16)
    spread = jnp.asarray(np.repeat(np.eye(span, dtype=np.float32), GROUP, axis=1), jnp.bfloat16)
    wide = jnp.einsum("hck,kn->hcn", shifted, spread, preferred_element_type=jnp.float32)
    same = (jnp.arange(channels)[:, None] % GROUP) == (jnp.arange(span * GROUP)[None, :] % GROUP)
    return jnp.where(same[None], wide, 0.0).astype(jnp.bfloat16)


def shifts(values, scratch):
    rows, group, lon = values.shape
    flat = values.reshape(rows * group, lon)
    wrapped = jnp.concatenate([flat[:, -RIM:], flat, flat[:, :RIM]], axis=1)
    for tap in range(KS):
        scratch[tap * rows * group : (tap + 1) * rows * group, :] = wrapped[:, tap : tap + lon]


def conv_kernel(above, own, below, band, out, scratch):
    rows, group, lon = own.shape
    shifts(jnp.concatenate([above[...], own[...], below[...]], axis=0), scratch)
    result = dot(band[...].reshape(rows * group, -1), scratch[...])
    out[...] = result.astype(out.dtype).reshape(rows, group, lon)


def tap_kernel(above, own, below, grads, parts, scratch):
    rows, group, lon = own.shape
    shifts(jnp.concatenate([above[...], own[...], below[...]], axis=0), scratch)
    pairs = dot_nt(grads[...].reshape(rows * group, lon), scratch[...])
    row = lax.broadcasted_iota(jnp.int32, pairs.shape, 0) % group
    col = lax.broadcasted_iota(jnp.int32, pairs.shape, 1) % group
    kept = jnp.where(row == col, pairs, 0.0)
    total = jnp.sum(kept[:group], axis=0, keepdims=True)
    for h in range(1, rows):
        line = jnp.sum(kept[h * group : (h + 1) * group], axis=0, keepdims=True)
        total += jnp.concatenate([line[:, h * group :], line[:, : h * group]], axis=1)
    parts[...] = total[None]


def back_kernel(above, own, below, cotangent, band, out, scratch):
    rows, group, lon = own.shape
    shifts(jnp.concatenate([above[...], own[...], below[...]], axis=0), scratch)
    spread = dot(band[...].reshape(rows * group, -1), scratch[...])
    total = cotangent[...].reshape(rows * group, lon).astype(jnp.float32) + spread
    out[...] = total.astype(out.dtype).reshape(rows, group, lon)


def pointwise_kernel(
    conv, fields, cotangent, mask, gain, shift, widen, widen_t, hidden_off, narrow, narrow_t, out_off,
    updated, conv_back, widen_part, narrow_part, gain_part, shift_part, hidden_part, out_part,
):
    lon = conv.shape[-1]

    @pl.when(pl.program_id(0) == 0)
    def _():
        for part in (widen_part, narrow_part, gain_part, shift_part, hidden_part, out_part):
            part[...] = jnp.zeros_like(part)

    f32, bf16 = jnp.float32, jnp.bfloat16
    step = 256
    for first in range(0, lon, step):
        cols = slice(first, min(first + step, lon))
        values = conv[0, :, cols].astype(f32)
        centre = jnp.mean(values, axis=0, keepdims=True)
        centred = values - centre
        inv_std = lax.rsqrt(jnp.mean(centred * centred, axis=0, keepdims=True) + EPSILON)
        normed = centred * inv_std
        scaled = (normed * gain[...] + shift[...]).astype(bf16)
        hidden = dot(widen_t[...], scaled) + hidden_off[...]
        cdf = 0.5 * (1.0 + lax.erf(hidden * (1.0 / math.sqrt(2.0))))
        active = (hidden * cdf).astype(bf16)
        slope = cdf + hidden * jnp.exp(-0.5 * hidden * hidden) * (1.0 / math.sqrt(2.0 * math.pi))
        ocean = mask[0, :, cols].astype(f32)
        branch = dot(narrow[...], active) + out_off[...]
        updated[0, :, cols] = (fields[0, :, cols].astype(f32) + ocean * branch).astype(bf16)
        upstream_wide = cotangent[0, :, cols].astype(f32) * ocean
        upstream = upstream_wide.astype(bf16)
        out_part[...] += jnp.sum(upstream_wide, axis=1, keepdims=True)
        narrow_part[...] += dot_nt(upstream, active)
        hidden_wide = dot(narrow_t[...], upstream) * slope
        hidden_back = hidden_wide.astype(bf16)
        hidden_part[...] += jnp.sum(hidden_wide, axis=1, keepdims=True)
        widen_part[...] += dot_nt(scaled, hidden_back)
        scaled_back = dot(widen[...], hidden_back)
        gain_part[...] += jnp.sum(scaled_back * normed, axis=1, keepdims=True)
        shift_part[...] += jnp.sum(scaled_back, axis=1, keepdims=True)
        normed_back = scaled_back * gain[...]
        conv_back[0, :, cols] = (
            inv_std
            * (
                normed_back
                - jnp.mean(normed_back, axis=0, keepdims=True)
                - normed * jnp.mean(normed_back * normed, axis=0, keepdims=True)
            )
        ).astype(bf16)


def halos(values, devices):
    def send(piece, pairs):
        piece = with_layout_constraint(piece, Layout(major_to_minor=(0, 1, 2)))
        piece = lax.ppermute(piece, "sp", pairs)
        return with_layout_constraint(piece, Layout(major_to_minor=(0, 1, 2)))

    above = send(values[-RIM:], [(d, d + 1) for d in range(devices - 1)])
    below = send(values[:RIM], [(d + 1, d) for d in range(devices - 1)])
    return above, below


def local(
    fields, cotangent, ocean_mask, kernel, norm_gain, norm_shift, widen, hidden_offset, narrow, output_offset
):
    devices = lax.axis_size("sp")
    samples, channels, rows, lon = cotangent.shape
    wide = widen.shape[1]
    f32, bf16 = jnp.float32, jnp.bfloat16
    grad_scale = 1.0 / math.sqrt(samples * rows * devices * lon)
    groups = channels // GROUP
    span = KS * (rows + KS - 1) * GROUP
    cost = pl.CostEstimate(
        flops=20 * rows * GROUP * span * lon * groups, bytes_accessed=4 * rows * channels * lon * 3, transcendentals=0
    )
    params = pltpu.CompilerParams(vmem_limit_bytes=48 * 1024 * 1024)

    band = band_matrix(kernel, rows)
    band_back = band_matrix(kernel[:, ::-1, ::-1], rows)
    cot_rows = jnp.swapaxes(cotangent[0], 0, 1)

    own = lax.all_to_all(fields, "sp", split_axis=2, concat_axis=1, tiled=True)
    own = jnp.swapaxes(own[0], 0, 1)
    above, below = halos(own, devices)

    def rows_spec(count):
        return pl.BlockSpec((count, GROUP, lon), lambda g: (0, g, 0))

    band_spec = pl.BlockSpec((rows, GROUP, span), lambda g: (0, g, 0))
    conv_out = pl.pallas_call(
        conv_kernel,
        name="depthwise",
        grid=(groups,),
        in_specs=[rows_spec(RIM), rows_spec(rows), rows_spec(RIM), band_spec],
        out_specs=rows_spec(rows),
        out_shape=jax.ShapeDtypeStruct((rows, channels, lon), bf16),
        scratch_shapes=[pltpu.VMEM((span, lon), bf16)],
        compiler_params=params,
    )(above, own, below, band)

    def row_spec(count):
        return pl.BlockSpec((1, count, lon), lambda h: (h, 0, 0))

    def whole(*shape):
        return pl.BlockSpec(shape, lambda h: (0,) * len(shape))

    column = lambda vector: vector[:, None]
    updated, conv_back, widen_part, narrow_part, gain_part, shift_part, hidden_part, out_part = pl.pallas_call(
        pointwise_kernel,
        name="pointwise",
        grid=(rows,),
        in_specs=[
            row_spec(channels), row_spec(channels), row_spec(channels), row_spec(1),
            whole(channels, 1), whole(channels, 1), whole(channels, wide), whole(wide, channels),
            whole(wide, 1), whole(channels, wide), whole(wide, channels), whole(channels, 1),
        ],
        out_specs=[
            row_spec(channels), row_spec(channels), whole(channels, wide), whole(channels, wide),
            whole(channels, 1), whole(channels, 1), whole(wide, 1), whole(channels, 1),
        ],
        out_shape=[
            jax.ShapeDtypeStruct((rows, channels, lon), bf16),
            jax.ShapeDtypeStruct((rows, channels, lon), bf16),
            jax.ShapeDtypeStruct((channels, wide), f32),
            jax.ShapeDtypeStruct((channels, wide), f32),
            jax.ShapeDtypeStruct((channels, 1), f32),
            jax.ShapeDtypeStruct((channels, 1), f32),
            jax.ShapeDtypeStruct((wide, 1), f32),
            jax.ShapeDtypeStruct((channels, 1), f32),
        ],
        compiler_params=params,
    )(
        conv_out, own, cot_rows, ocean_mask[:, None, :], column(norm_gain), column(norm_shift),
        widen, widen.T, column(hidden_offset), narrow, narrow.T, column(output_offset),
    )

    g_above, g_below = halos(conv_back, devices)
    pairs = pl.pallas_call(
        tap_kernel,
        name="tap_grads",
        grid=(groups,),
        in_specs=[rows_spec(RIM), rows_spec(rows), rows_spec(RIM), rows_spec(rows)],
        out_specs=pl.BlockSpec((1, 1, span), lambda g: (g, 0, 0)),
        out_shape=jax.ShapeDtypeStruct((groups, 1, span), f32),
        scratch_shapes=[pltpu.VMEM((span, lon), bf16)],
        compiler_params=params,
        cost_estimate=cost,
    )(above, own, below, conv_back)

    taps = pairs.reshape(groups, KS, rows + KS - 1, GROUP)[:, :, :KS]
    kernel_part = jnp.transpose(taps, (0, 3, 2, 1)).reshape(channels, KS * KS)
    small = jnp.concatenate([gain_part[:, 0], shift_part[:, 0], hidden_part[:, 0], out_part[:, 0]])
    pieces = [
        part.reshape(devices, -1)
        for part in (widen_part, narrow_part, jnp.pad(kernel_part, ((0, 0), (0, 128 - KS * KS))))
    ]
    pieces.append(jnp.broadcast_to(small[None], (devices, small.shape[0])))
    joined = jnp.concatenate([piece.reshape(devices, -1, 128) for piece in pieces], axis=1)
    joined = lax.all_to_all(joined, "sp", split_axis=0, concat_axis=0, tiled=True)
    summed = jnp.sum(joined, axis=0) * grad_scale

    grad_rows = pl.pallas_call(
        back_kernel,
        name="depthwise_back",
        grid=(groups,),
        in_specs=[rows_spec(RIM), rows_spec(rows), rows_spec(RIM), rows_spec(rows), band_spec],
        out_specs=rows_spec(rows),
        out_shape=jax.ShapeDtypeStruct((rows, channels, lon), bf16),
        scratch_shapes=[pltpu.VMEM((span, lon), bf16)],
        compiler_params=params,
        cost_estimate=cost,
    )(g_above, conv_back, g_below, cot_rows, band_back)

    fields_grad = lax.all_to_all(
        jnp.swapaxes(grad_rows, 0, 1)[None], "sp", split_axis=1, concat_axis=2, tiled=True
    )

    own_channels = channels // devices
    edges = np.cumsum([own_channels * wide // 128, own_channels * wide // 128, own_channels])
    widen_sum, narrow_sum, kernel_sum, small_sum = jnp.split(summed, edges)
    small_sum = small_sum.reshape(-1)
    gain_sum, shift_sum, hidden_sum, output_sum = jnp.split(small_sum, np.cumsum([channels, channels, wide]))
    return (
        jnp.swapaxes(updated, 0, 1)[None],
        fields_grad,
        kernel_sum[:, : KS * KS].reshape(-1, KS, KS),
        widen_sum.reshape(-1, wide),
        narrow_sum.reshape(-1, wide),
        gain_sum,
        shift_sum,
        hidden_sum,
        output_sum,
    )


def solution(mesh):
    return jax.shard_map(
        local,
        mesh=mesh,
        in_specs=(
            P("groups", "sp", None, None),
            P("groups", None, "sp", None),
            P("sp", None),
            P("groups", None, None),
            P("groups"),
            P("groups"),
            P("groups", None),
            P("groups"),
            P("groups", None),
            P("groups"),
        ),
        out_specs=(
            P("groups", None, "sp", None),
            P("groups", "sp", None, None),
            P(("groups", "sp"), None, None),
            P(("groups", "sp"), None),
            P(("groups", "sp"), None),
            P("groups"),
            P("groups"),
            P("groups"),
            P("groups"),
        ),
        check_vma=False,
    )
```

```python
import functools
import math

import jax
import jax.numpy as jnp
import numpy as np
from jax import lax
from jax.experimental import pallas as pl
from jax.experimental.pallas import tpu as pltpu
from jax.sharding import PartitionSpec as P

KS = 7
RIM = KS // 2
EPSILON = 1e-06
GROUP = 16
NT = (((1,), (1,)), ((), ()))


def dot(former, latter):
    return jnp.dot(former, latter, preferred_element_type=jnp.float32)


def dot_nt(former, latter):
    return lax.dot_general(former, latter, NT, preferred_element_type=jnp.float32)


def band_matrix(kernel, rows):
    channels = kernel.shape[0]
    taps = jnp.swapaxes(kernel, 1, 2)
    shifted = jnp.stack([jnp.pad(taps, ((0, 0), (0, 0), (h, rows - 1 - h))) for h in range(rows)])
    span = KS * (rows + KS - 1)
    shifted = shifted.reshape(rows, channels, span).astype(jnp.bfloat16)
    spread = jnp.asarray(np.repeat(np.eye(span, dtype=np.float32), GROUP, axis=1), jnp.bfloat16)
    wide = jnp.einsum("hck,kn->hcn", shifted, spread, preferred_element_type=jnp.float32)
    same = (jnp.arange(channels)[:, None] % GROUP) == (jnp.arange(span * GROUP)[None, :] % GROUP)
    return jnp.where(same[None], wide, 0.0).astype(jnp.bfloat16)


def shifts(values, scratch):
    rows, group, lon = values.shape
    flat = values.reshape(rows * group, lon)
    wrapped = jnp.concatenate([flat[:, -RIM:], flat, flat[:, :RIM]], axis=1)
    for tap in range(KS):
        scratch[tap * rows * group : (tap + 1) * rows * group, :] = wrapped[:, tap : tap + lon]


def conv_kernel(above, own, below, band, out, scratch):
    rows, group, lon = own.shape
    shifts(jnp.concatenate([above[:, :, :lon], own[...], below[:, :, :lon]], axis=0), scratch)
    result = dot(band[...].reshape(rows * group, -1), scratch[...])
    out[...] = result.astype(out.dtype).reshape(rows, group, lon)


def tap_kernel(above, own, below, grads, parts, scratch):
    rows, group, lon = own.shape
    shifts(jnp.concatenate([above[:, :, :lon], own[...], below[:, :, :lon]], axis=0), scratch)
    pairs = dot_nt(grads[...].reshape(rows * group, lon), scratch[...])
    row = lax.broadcasted_iota(jnp.int32, pairs.shape, 0) % group
    col = lax.broadcasted_iota(jnp.int32, pairs.shape, 1) % group
    kept = jnp.where(row == col, pairs, 0.0)
    total = jnp.sum(kept[:group], axis=0, keepdims=True)
    for h in range(1, rows):
        line = jnp.sum(kept[h * group : (h + 1) * group], axis=0, keepdims=True)
        total += jnp.concatenate([line[:, h * group :], line[:, : h * group]], axis=1)
    parts[...] = total[None]


def back_kernel(above, own, below, cotangent, band, out, scratch):
    rows, group, lon = own.shape
    shifts(jnp.concatenate([above[:, :, :lon], own[...], below[:, :, :lon]], axis=0), scratch)
    spread = dot(band[...].reshape(rows * group, -1), scratch[...])
    total = cotangent[...].reshape(rows * group, lon).astype(jnp.float32) + spread
    out[...] = total.astype(out.dtype).reshape(rows, group, lon)


def pointwise_kernel(
    conv, fields, cotangent, mask, gain, shift, widen, widen_t, hidden_off, narrow, narrow_t, out_off,
    updated, conv_back, widen_part, narrow_part, gain_part, shift_part, hidden_part, out_part,
):
    lon = conv.shape[-1]

    @pl.when(pl.program_id(0) == 0)
    def _():
        for part in (widen_part, narrow_part, gain_part, shift_part, hidden_part, out_part):
            part[...] = jnp.zeros_like(part)

    f32, bf16 = jnp.float32, jnp.bfloat16
    step = 256
    for first in range(0, lon, step):
        cols = slice(first, min(first + step, lon))
        values = conv[0, :, cols].astype(f32)
        centre = jnp.mean(values, axis=0, keepdims=True)
        centred = values - centre
        inv_std = lax.rsqrt(jnp.mean(centred * centred, axis=0, keepdims=True) + EPSILON)
        normed = centred * inv_std
        scaled = (normed * gain[...] + shift[...]).astype(bf16)
        hidden = dot(widen_t[...], scaled) + hidden_off[...]
        cdf = 0.5 * (1.0 + lax.erf(hidden * (1.0 / math.sqrt(2.0))))
        active = (hidden * cdf).astype(bf16)
        slope = cdf + hidden * jnp.exp(-0.5 * hidden * hidden) * (1.0 / math.sqrt(2.0 * math.pi))
        ocean = mask[0, :, cols].astype(f32)
        branch = dot(narrow[...], active) + out_off[...]
        updated[0, :, cols] = (fields[0, :, cols].astype(f32) + ocean * branch).astype(bf16)
        upstream_wide = cotangent[0, :, cols].astype(f32) * ocean
        upstream = upstream_wide.astype(bf16)
        out_part[...] += jnp.sum(upstream_wide, axis=1, keepdims=True)
        narrow_part[...] += dot_nt(upstream, active)
        hidden_wide = dot(narrow_t[...], upstream) * slope
        hidden_back = hidden_wide.astype(bf16)
        hidden_part[...] += jnp.sum(hidden_wide, axis=1, keepdims=True)
        widen_part[...] += dot_nt(scaled, hidden_back)
        scaled_back = dot(widen[...], hidden_back)
        gain_part[...] += jnp.sum(scaled_back * normed, axis=1, keepdims=True)
        shift_part[...] += jnp.sum(scaled_back, axis=1, keepdims=True)
        normed_back = scaled_back * gain[...]
        conv_back[0, :, cols] = (
            inv_std
            * (
                normed_back
                - jnp.mean(normed_back, axis=0, keepdims=True)
                - normed * jnp.mean(normed_back * normed, axis=0, keepdims=True)
            )
        ).astype(bf16)


def halos(values, devices):
    def send(piece, pairs):
        piece = jnp.pad(piece, ((0, 0), (0, 0), (0, -piece.shape[2] % 128)))
        return lax.ppermute(piece, "sp", pairs)

    above = send(values[-RIM:], [(d, d + 1) for d in range(devices - 1)])
    below = send(values[:RIM], [(d + 1, d) for d in range(devices - 1)])
    return above, below


def local(
    fields, cotangent, ocean_mask, kernel, norm_gain, norm_shift, widen, hidden_offset, narrow, output_offset
):
    devices = lax.axis_size("sp")
    samples, channels, rows, lon = cotangent.shape
    wide = widen.shape[1]
    f32, bf16 = jnp.float32, jnp.bfloat16
    grad_scale = 1.0 / math.sqrt(samples * rows * devices * lon)
    groups = channels // GROUP
    span = KS * (rows + KS - 1) * GROUP
    cost = pl.CostEstimate(
        flops=20 * rows * GROUP * span * lon * groups, bytes_accessed=4 * rows * channels * lon * 3, transcendentals=0
    )
    params = pltpu.CompilerParams(vmem_limit_bytes=48 * 1024 * 1024)

    band = band_matrix(kernel, rows)
    band_back = band_matrix(kernel[:, ::-1, ::-1], rows)
    cot_rows = jnp.swapaxes(cotangent[0], 0, 1)

    own = lax.all_to_all(fields, "sp", split_axis=2, concat_axis=1, tiled=True)
    own = jnp.swapaxes(own[0], 0, 1)
    above, below = halos(own, devices)

    def rows_spec(count):
        return pl.BlockSpec((count, GROUP, lon), lambda g: (0, g, 0))

    halo_spec = pl.BlockSpec((RIM, GROUP, above.shape[2]), lambda g: (0, g, 0))
    band_spec = pl.BlockSpec((rows, GROUP, span), lambda g: (0, g, 0))
    conv_out = pl.pallas_call(
        conv_kernel,
        name="depthwise",
        grid=(groups,),
        in_specs=[halo_spec, rows_spec(rows), halo_spec, band_spec],
        out_specs=rows_spec(rows),
        out_shape=jax.ShapeDtypeStruct((rows, channels, lon), bf16),
        scratch_shapes=[pltpu.VMEM((span, lon), bf16)],
        compiler_params=params,
    )(above, own, below, band)

    def row_spec(count):
        return pl.BlockSpec((1, count, lon), lambda h: (h, 0, 0))

    def whole(*shape):
        return pl.BlockSpec(shape, lambda h: (0,) * len(shape))

    column = lambda vector: vector[:, None]
    updated, conv_back, widen_part, narrow_part, gain_part, shift_part, hidden_part, out_part = pl.pallas_call(
        pointwise_kernel,
        name="pointwise",
        grid=(rows,),
        in_specs=[
            row_spec(channels), row_spec(channels), row_spec(channels), row_spec(1),
            whole(channels, 1), whole(channels, 1), whole(channels, wide), whole(wide, channels),
            whole(wide, 1), whole(channels, wide), whole(wide, channels), whole(channels, 1),
        ],
        out_specs=[
            row_spec(channels), row_spec(channels), whole(channels, wide), whole(channels, wide),
            whole(channels, 1), whole(channels, 1), whole(wide, 1), whole(channels, 1),
        ],
        out_shape=[
            jax.ShapeDtypeStruct((rows, channels, lon), bf16),
            jax.ShapeDtypeStruct((rows, channels, lon), bf16),
            jax.ShapeDtypeStruct((channels, wide), f32),
            jax.ShapeDtypeStruct((channels, wide), f32),
            jax.ShapeDtypeStruct((channels, 1), f32),
            jax.ShapeDtypeStruct((channels, 1), f32),
            jax.ShapeDtypeStruct((wide, 1), f32),
            jax.ShapeDtypeStruct((channels, 1), f32),
        ],
        compiler_params=params,
    )(
        conv_out, own, cot_rows, ocean_mask[:, None, :], column(norm_gain), column(norm_shift),
        widen, widen.T, column(hidden_offset), narrow, narrow.T, column(output_offset),
    )

    g_above, g_below = halos(conv_back, devices)
    pairs = pl.pallas_call(
        tap_kernel,
        name="tap_grads",
        grid=(groups,),
        in_specs=[halo_spec, rows_spec(rows), halo_spec, rows_spec(rows)],
        out_specs=pl.BlockSpec((1, 1, span), lambda g: (g, 0, 0)),
        out_shape=jax.ShapeDtypeStruct((groups, 1, span), f32),
        scratch_shapes=[pltpu.VMEM((span, lon), bf16)],
        compiler_params=params,
        cost_estimate=cost,
    )(above, own, below, conv_back)

    taps = pairs.reshape(groups, KS, rows + KS - 1, GROUP)[:, :, :KS]
    kernel_part = jnp.transpose(taps, (0, 3, 2, 1)).reshape(channels, KS * KS)
    small = jnp.concatenate([gain_part[:, 0], shift_part[:, 0], hidden_part[:, 0], out_part[:, 0]])
    pieces = [
        part.reshape(devices, -1)
        for part in (widen_part, narrow_part, jnp.pad(kernel_part, ((0, 0), (0, 128 - KS * KS))))
    ]
    pieces.append(jnp.broadcast_to(small[None], (devices, small.shape[0])))
    joined = jnp.concatenate([piece.reshape(devices, -1, 128) for piece in pieces], axis=1)
    joined = lax.all_to_all(joined, "sp", split_axis=0, concat_axis=0, tiled=True)
    summed = jnp.sum(joined, axis=0) * grad_scale

    grad_rows = pl.pallas_call(
        back_kernel,
        name="depthwise_back",
        grid=(groups,),
        in_specs=[halo_spec, rows_spec(rows), halo_spec, rows_spec(rows), band_spec],
        out_specs=rows_spec(rows),
        out_shape=jax.ShapeDtypeStruct((rows, channels, lon), bf16),
        scratch_shapes=[pltpu.VMEM((span, lon), bf16)],
        compiler_params=params,
        cost_estimate=cost,
    )(g_above, conv_back, g_below, cot_rows, band_back)

    fields_grad = lax.all_to_all(
        jnp.swapaxes(grad_rows, 0, 1)[None], "sp", split_axis=1, concat_axis=2, tiled=True
    )

    own_channels = channels // devices
    edges = np.cumsum([own_channels * wide // 128, own_channels * wide // 128, own_channels])
    widen_sum, narrow_sum, kernel_sum, small_sum = jnp.split(summed, edges)
    small_sum = small_sum.reshape(-1)
    gain_sum, shift_sum, hidden_sum, output_sum = jnp.split(small_sum, np.cumsum([channels, channels, wide]))
    return (
        jnp.swapaxes(updated, 0, 1)[None],
        fields_grad,
        kernel_sum[:, : KS * KS].reshape(-1, KS, KS),
        widen_sum.reshape(-1, wide),
        narrow_sum.reshape(-1, wide),
        gain_sum,
        shift_sum,
        hidden_sum,
        output_sum,
    )


def solution(mesh):
    return jax.shard_map(
        local,
        mesh=mesh,
        in_specs=(
            P("groups", "sp", None, None),
            P("groups", None, "sp", None),
            P("sp", None),
            P("groups", None, None),
            P("groups"),
            P("groups"),
            P("groups", None),
            P("groups"),
            P("groups", None),
            P("groups"),
        ),
        out_specs=(
            P("groups", None, "sp", None),
            P("groups", "sp", None, None),
            P(("groups", "sp"), None, None),
            P(("groups", "sp"), None),
            P(("groups", "sp"), None),
            P("groups"),
            P("groups"),
            P("groups"),
            P("groups"),
        ),
        check_vma=False,
    )
```
